512 devices in a mesh: section: 2 (over core), blk: 32 (over z, y_lo), head: 8 (over y_hi, x).
Axes of the slice: x: 4, y: 8 (y_hi: 2, y_lo: 4; y = y_hi * 4 + y_lo), z: 8, core: 2. Of those that a mesh axis runs over, the one named last changes fastest.
Arguments:
- queries: bfloat16 [2, 8192, 8192], P('section', ('blk', 'head')), may hold values from -96 to 96
- key_vectors: bfloat16 [2, 8192, 1024], P('section', ('blk', 'head')), may hold values from -6 to 6
- value_vectors: bfloat16 [2, 8192, 1024], P('section', ('blk', 'head')), may hold values from -6 to 6
- residual: bfloat16 [8192, 8192], P('blk', 'head'), may hold values from -128 to 128
- pair_order: int32 [32], replicated, may hold values from 0 to 31, as said below
- probe_gain: float32 [2, 8192], P('section', 'head'), may hold values from 0.1 to 1.9
- probe_weight: float32 [2, 8192], P('section', 'head'), may hold values from -0.0625 to 0.0625
Outputs:
- hidden_out: bfloat16 [2, 8192, 8192], P('section', 'blk', 'head')
- rewards: float32 [2, 8192], P('section', 'blk')
The draws below stay inside these ranges and needn't reach their ends.
Inputs may be any that keep to these rules, and one draw needn't show every extreme that they name: `pair_order`: each value appears once.
All inputs are finite; a program needn't handle non-finite values.
Results may differ from the reference program's by a relative error of at most 0.004.
Values may be sent and summed in bfloat16 or wider, within the bound.
No kernel may reach another device: no remote copies, remote signals or barrier semaphores. Data moves between devices by JAX's collectives and lax.ppermute only.
A program may use at most 64 MiB of HBM per device.

```python
import jax
import jax.numpy as jnp
from jax import lax

D = 8192
HEADS = 64
KV_HEADS = 8
HEAD_DIM = 128
TOK_BLK = 256
TOKENS = 8192
LAYERS = 2
N_BLK = 32


def block_order(key):
    return jax.random.permutation(jax.random.fold_in(key, 11), N_BLK).astype(jnp.int32)


def draw_pair_order(key, part):
    return block_order(key)


def draw_key_vectors(key, part):
    base = jax.random.normal(jax.random.fold_in(key, 31), (LAYERS, TOKENS, KV_HEADS * HEAD_DIM), jnp.float32)
    base = jnp.clip(base, -6.0, 6.0)
    return base.astype(jnp.bfloat16)


def draw_queries(key, part):
    base = jax.random.normal(jax.random.fold_in(key, 33), (LAYERS, TOKENS, D), jnp.float32)
    base = jnp.clip(base, -6.0, 6.0)
    return base.astype(jnp.bfloat16)


def draw_residual(key, part):
    noise = jax.random.normal(jax.random.fold_in(key, 41), (TOKENS, D), jnp.float32)
    noise = jnp.clip(noise, -6.0, 6.0)
    columns = jnp.arange(D, dtype=jnp.float32) / D
    result = noise * jnp.power(3.0, 0.5 * columns)[None, :]
    return jnp.clip(result, -128.0, 128.0).astype(jnp.bfloat16)


def block_scale(key, shape, shards, low, top_value):
    factor_of = 1.0
    for dim, shards_of in shards:
        heights = jax.random.uniform(jax.random.fold_in(jax.random.fold_in(key, 6), dim), (shards_of,), jnp.float32, low / len(shards), top_value / len(shards))
        factor_of = factor_of * jnp.repeat(jnp.exp(heights), shape[dim] // shards_of).reshape((-1,) + (1,) * (len(shape) - 1 - dim))
    return factor_of


def centred(stream_key, shape, width, bound, shards=(), held_as=jnp.bfloat16):
    drawn = width * jax.random.normal(stream_key, shape, jnp.float32)
    if shards:
        drawn = drawn * block_scale(stream_key, shape, shards, -0.22, 0.18)
    return jnp.clip(drawn, -bound, bound).astype(held_as)


def setup_inputs(seed: int = 0) -> dict:
    streams_of = jax.random.split(jax.random.key(seed), 8)
    return {
        "queries": draw_queries(jax.random.fold_in(streams_of[7], 71), 0),
        "key_vectors": draw_key_vectors(jax.random.fold_in(streams_of[7], 71), 0),
        "value_vectors": centred(streams_of[2], (LAYERS, TOKENS, KV_HEADS * HEAD_DIM), 1.0, 6.0, ((0, 2), (1, 256))),
        "residual": draw_residual(jax.random.fold_in(streams_of[7], 71), 0),
        "pair_order": draw_pair_order(jax.random.fold_in(streams_of[7], 71), 0),
        "probe_gain": jnp.clip(1.0 + 0.18 * jax.random.normal(streams_of[5], (LAYERS, D), jnp.float32), 0.1, 1.9),
        "probe_weight": centred(streams_of[6], (LAYERS, D), D ** -0.5, 0.0625, ((0, 2), (1, 8)), jnp.float32),
    }


def token_positions(pair_order):
    span_rows = TOK_BLK // 2
    row_index = jnp.arange(TOKENS, dtype=jnp.int32)
    shard = row_index // TOK_BLK
    within = row_index % TOK_BLK
    lower = pair_order[shard].astype(jnp.int32)
    which = jnp.where(within < span_rows, lower, 2 * N_BLK - 1 - lower)
    return (which * span_rows + within % span_rows).astype(jnp.int32)

def attention(queries, key_vectors, value_vectors, positions):
    group = HEADS // KV_HEADS
    factor = HEAD_DIM ** (-0.5)
    causal = positions[None, :] <= positions[:, None]

    def one_head(head):
        q_head = lax.dynamic_slice_in_dim(queries, head * HEAD_DIM, HEAD_DIM, 1)
        offset = head // group * HEAD_DIM
        k_head = lax.dynamic_slice_in_dim(key_vectors, offset, HEAD_DIM, 1)
        v_head = lax.dynamic_slice_in_dim(value_vectors, offset, HEAD_DIM, 1)
        scores = jnp.dot(q_head, k_head.T, preferred_element_type=jnp.float32) * factor
        scores = jnp.where(causal, scores, -jnp.inf)
        largest = lax.optimization_barrier(jnp.max(scores, axis=1, keepdims=True))
        weights = jnp.exp(scores - largest)
        totals = lax.optimization_barrier(jnp.sum(weights, axis=1, keepdims=True))
        mixed = jnp.dot(weights.astype(jnp.bfloat16), v_head, preferred_element_type=jnp.float32)
        return mixed / totals
    stacked = lax.map(one_head, jnp.arange(HEADS, dtype=jnp.int32))
    return jnp.transpose(stacked, (1, 0, 2)).reshape(TOKENS, D)

def reference(queries, key_vectors, value_vectors, residual, pair_order, probe_gain, probe_weight):
    positions = token_positions(pair_order)
    stream = residual
    hidden = []
    rewards = []
    for layer in range(LAYERS):
        attended = attention(queries[layer], key_vectors[layer], value_vectors[layer], positions)
        stream = (stream.astype(jnp.float32) + attended).astype(jnp.bfloat16)
        widened = stream.astype(jnp.float32)
        squares = lax.optimization_barrier(jnp.mean(widened * widened, axis=-1))
        products = lax.optimization_barrier(jnp.sum(widened * probe_gain[layer] * probe_weight[layer], axis=-1))
        rewards.append(products * lax.rsqrt(squares + 1e-05))
        hidden.append(stream)
    return (jnp.stack(hidden), jnp.stack(rewards))
```

```python
import functools
import math

import jax
import jax.numpy as jnp
from jax import lax
from jax.experimental import pallas as pl
from jax.experimental.pallas import tpu as pltpu
from jax.sharding import Mesh, PartitionSpec as P

D = 8192
HEADS = 64
KV_HEADS = 8
HEAD_DIM = 128
HALF = 128
GROUP = HEADS // KV_HEADS
ROWS = HALF * GROUP
TILE = 256

NEG = -1e30
SCALE = HEAD_DIM ** (-0.5) * math.log2(math.e)

HEAD = ("yhi", "x")


def fold(q_ref, m_ref, l_ref, a_ref, half, keys, values, masked=False):
    count = keys.shape[0]

    def tile(t, _):
        rows = pl.ds(pl.multiple_of(t * TILE, TILE), TILE)
        s = lax.dot_general(
            q_ref[half, rows], keys, (((1,), (1,)), ((), ())), preferred_element_type=jnp.float32
        )
        if masked:
            r = lax.broadcasted_iota(jnp.int32, s.shape, 0) % HALF
            k = lax.broadcasted_iota(jnp.int32, s.shape, 1)
            s = jnp.where(k <= r, s, NEG)
        parts = [s[:, j : j + 128] for j in range(0, count, 128)]
        top = functools.reduce(jnp.maximum, parts)
        old = m_ref[half, rows]
        new = jnp.maximum(old, jnp.max(top, axis=1, keepdims=True))
        keep = jnp.exp2((old - new) * SCALE)
        weights = [jnp.exp2((p - new) * SCALE) for p in parts]
        l_ref[half, rows] = l_ref[half, rows] * keep + functools.reduce(jnp.add, weights)
        w = jnp.concatenate([p.astype(jnp.bfloat16) for p in weights], axis=1)
        a_ref[half, rows] = a_ref[half, rows] * keep + jnp.dot(
            w, values, preferred_element_type=jnp.float32
        )
        m_ref[half, rows] = new
        return 0

    lax.fori_loop(0, ROWS // TILE, tile, 0)


def attend(first, n, info_ref, q_ref, *refs):
    chunks, state = refs[:n], refs[n:]
    if first:
        m_ref, l_ref, a_ref = state
        m_ref[...] = jnp.full(m_ref.shape, NEG, jnp.float32)
        l_ref[...] = jnp.zeros(l_ref.shape, jnp.float32)
        a_ref[...] = jnp.zeros(a_ref.shape, jnp.float32)
    else:
        m_in, l_in, a_in, m_ref, l_ref, a_ref = state
        m_ref[...] = m_in[...]
        l_ref[...] = l_in[...]
        a_ref[...] = a_in[...]
    own = info_ref[0]
    run = functools.partial(fold, q_ref, m_ref, l_ref, a_ref)
    at = 1
    for chunk in chunks:
        pairs = chunk.shape[0] // (2 * HALF)
        lows = [chunk[i * 256 : i * 256 + 128] for i in range(pairs)]
        low = jnp.concatenate(lows, axis=0)
        run(1, low[:, :128], low[:, 128:])
        for i in range(pairs):
            their = info_ref[at]
            at += 1
            later = (their > own).astype(jnp.int32)

            def other(later=later, i=i, chunk=chunk):
                rows = pl.ds(pl.multiple_of(i * 256 + later * 128, 128), 128)
                run(later, chunk[rows, :128], chunk[rows, 128:])

            if first:
                pl.when(their != own)(other)

                @pl.when(their == own)
                def _(i=i, chunk=chunk):
                    for half in range(2):
                        rows = slice(i * 256 + half * 128, i * 256 + half * 128 + 128)
                        run(half, chunk[rows, :128], chunk[rows, 128:], masked=True)
            else:
                other()


def attention(info, q, chunks, state):
    first = state is None
    n = len(chunks)
    tokens = sum(c.shape[0] for c in chunks)
    shape = jax.ShapeDtypeStruct((2, ROWS, HEAD_DIM), jnp.float32)
    vmem = pl.BlockSpec(memory_space=pltpu.VMEM)
    operands = (info, q, *chunks) + (() if first else tuple(state))
    return pl.pallas_call(
        functools.partial(attend, first, n),
        out_shape=(shape,) * 3,
        in_specs=[pl.BlockSpec(memory_space=pltpu.SMEM)] + [vmem] * (len(operands) - 1),
        out_specs=(vmem,) * 3,
        input_output_aliases={} if first else {2 + n + k: k for k in range(3)},
        cost_estimate=pl.CostEstimate(
            flops=4 * ROWS * tokens * HEAD_DIM * 4,
            bytes_accessed=tokens * 512,
            transcendentals=ROWS * tokens,
        ),
        compiler_params=pltpu.CompilerParams(vmem_limit_bytes=48 * 1024 * 1024),
        name="attend_first" if first else "attend_next",
    )(*operands)


def finish(l_ref, a_ref, residual_ref, att_ref, own_ref):
    for half in range(2):
        for h in range(GROUP):
            rows = slice(h * HALF, (h + 1) * HALF)
            total = jnp.sum(l_ref[half, rows], axis=1, keepdims=True)
            att = a_ref[half, rows] / total
            to = (slice(half * HALF, (half + 1) * HALF), slice(h * HEAD_DIM, (h + 1) * HEAD_DIM))
            att_ref[to] = att
            own_ref[to] = (residual_ref[to].astype(jnp.float32) + att).astype(jnp.bfloat16)


def finished(totals, accum, residual):
    vmem = pl.BlockSpec(memory_space=pltpu.VMEM)
    return pl.pallas_call(
        finish,
        out_shape=(
            jax.ShapeDtypeStruct(residual.shape, jnp.float32),
            jax.ShapeDtypeStruct(residual.shape, jnp.bfloat16),
        ),
        in_specs=[vmem] * 3,
        out_specs=(vmem,) * 2,
        cost_estimate=pl.CostEstimate(flops=1 << 19, bytes_accessed=1 << 22, transcendentals=0),
        compiler_params=pltpu.CompilerParams(vmem_limit_bytes=32 * 1024 * 1024),
        name="finish",
    )(totals, accum, residual)


def body(queries, key_vectors, value_vectors, residual, pair_order, probe_gain, probe_weight):
    heads = 8
    nz, ny = lax.axis_size("z"), lax.axis_size("ylo")
    z = lax.axis_index("z")
    tokens = key_vectors.shape[1]

    k = key_vectors[0].reshape(tokens, heads, HEAD_DIM)
    v = value_vectors[0].reshape(tokens, heads, HEAD_DIM)
    kv = jnp.concatenate([k, v], axis=2).transpose(1, 0, 2)
    sent = jnp.broadcast_to(kv[None], (ny, heads, tokens, 2 * HEAD_DIM))
    sent = sent.reshape(ny * heads, tokens, 2 * HEAD_DIM)
    mine = lax.all_to_all(sent, ("ylo", *HEAD), split_axis=0, concat_axis=0, tiled=True)
    mine = mine.reshape(ny * heads * tokens, 2 * HEAD_DIM)

    q = queries[0].reshape(tokens, heads, GROUP * HEAD_DIM).transpose(1, 0, 2)

    def shift(x, by):
        return lax.ppermute(x, "z", [(i, (i + by) % nz) for i in range(nz)])

    left1, right1 = shift(mine, 1), shift(mine, -1)
    q = lax.all_to_all(q, HEAD, split_axis=0, concat_axis=0, tiled=True)
    q = q.reshape(2, HALF, GROUP, HEAD_DIM).transpose(0, 2, 1, 3).reshape(2, ROWS, HEAD_DIM)

    left2, right2 = shift(left1, 1), shift(right1, -1)
    left3, right3 = shift(left2, 1), shift(right2, -1)
    cut = left3.shape[0] // 2
    left4, right4 = shift(left3[:cut], 1), shift(right3[cut:], -1)

    table = pair_order.reshape(nz, ny)
    row = lax.broadcasted_iota(jnp.int32, (nz, ny), 0)
    column = lax.broadcasted_iota(jnp.int32, (nz, ny), 1)
    own = jnp.sum(jnp.where((row == z) & (column == lax.axis_index("ylo")), table, 0))

    def pairs_of(offset):
        return jnp.sum(jnp.where(row == (z + offset + nz) % nz, table, 0), axis=0)

    def info(*pieces):
        return jnp.concatenate([own[None], *pieces])

    state = attention(info(pairs_of(0)), q, (mine,), None)
    state = attention(info(pairs_of(-1), pairs_of(1)), q, (left1, right1), state)
    state = attention(info(pairs_of(-2), pairs_of(2)), q, (left2, right2), state)
    state = attention(info(pairs_of(-3), pairs_of(3)), q, (left3, right3), state)
    last = pairs_of(4)
    state = attention(info(last), q, (left4, right4), state)

    attended, own_stream = finished(state[1], state[2], residual)
    handed = lax.ppermute(own_stream, "section", [(0, 1)])
    later_stream = (handed.astype(jnp.float32) + attended).astype(jnp.bfloat16)
    stream = jnp.where(lax.axis_index("section") == 0, own_stream, later_stream)
    widened = stream.astype(jnp.float32)
    squares = jnp.sum(widened * widened, axis=-1)
    products = jnp.sum(widened * probe_gain[0][None, :] * probe_weight[0][None, :], axis=-1)
    both = jnp.stack([squares, products])
    copies = jnp.broadcast_to(both[None], (heads, *both.shape))
    both = jnp.sum(lax.all_to_all(copies, HEAD, split_axis=0, concat_axis=0, tiled=True), axis=0)
    reward = both[1] * lax.rsqrt(both[0] / D + 1e-05)
    return (stream[None], reward[None])


def solution(mesh):
    fine = Mesh(mesh.devices.reshape(2, 8, 4, 2, 4), ("section", "z", "ylo", "yhi", "x"))
    rows = ("z", "ylo", "yhi", "x")
    return jax.shard_map(
        body,
        mesh=fine,
        in_specs=(
            P("section", rows, None),
            P("section", rows, None),
            P("section", rows, None),
            P(("z", "ylo"), HEAD),
            P(),
            P("section", HEAD),
            P("section", HEAD),
        ),
        out_specs=(P("section", ("z", "ylo"), HEAD), P("section", ("z", "ylo"))),
        check_vma=False,
    )
```

```python
import functools
import math

import jax
import jax.numpy as jnp
from jax import lax
from jax.experimental import pallas as pl
from jax.experimental.pallas import tpu as pltpu
from jax.sharding import Mesh, PartitionSpec as P

D = 8192
HEADS = 64
KV_HEADS = 8
HEAD_DIM = 128
HALF = 128
GROUP = HEADS // KV_HEADS
ROWS = HALF * GROUP
TILE = 256

NEG = -1e30
SCALE = HEAD_DIM ** (-0.5) * math.log2(math.e)

HEAD = ("yhi", "x")


def scored(q_ref, s_ref, half, t, keys):
    rows = slice(t * TILE, (t + 1) * TILE)
    s_ref[:, : keys.shape[0]] = lax.dot_general(
        q_ref[half, rows], keys, (((1,), (1,)), ((), ())), preferred_element_type=jnp.float32
    )


def folded(s_ref, state, fresh, half, t, values, offsets, diagonal):
    rows = slice(t * TILE, (t + 1) * TILE)
    m_in, l_in, a_in, m_ref, l_ref, a_ref = state
    parts = []
    for j, offset in enumerate(offsets):
        p = s_ref[:, j * 128 : (j + 1) * 128]
        if offset is not None:
            p = p + offset
        if diagonal is not None and diagonal[j] is not None:
            r = lax.broadcasted_iota(jnp.int32, p.shape, 0) % HALF
            k = lax.broadcasted_iota(jnp.int32, p.shape, 1)
            p = jnp.where(k <= r + diagonal[j], p, NEG)
        parts.append(p)
    top = functools.reduce(jnp.maximum, parts)
    top = jnp.max(top, axis=1, keepdims=True)
    if fresh:
        new = jnp.broadcast_to(jnp.maximum(top, NEG), (TILE, 128))
    else:
        old = m_in[half, rows]
        new = jnp.maximum(old, top)
        keep = jnp.exp2((old - new) * SCALE)
    weights = [jnp.exp2((p - new) * SCALE) for p in parts]
    total = functools.reduce(jnp.add, weights)
    w = jnp.concatenate([p.astype(jnp.bfloat16) for p in weights], axis=1)
    mixed = jnp.dot(w, values, preferred_element_type=jnp.float32)
    m_ref[half, rows] = new
    if fresh:
        l_ref[half, rows] = total
        a_ref[half, rows] = mixed
    else:
        l_ref[half, rows] = l_in[half, rows] * keep + total
        a_ref[half, rows] = a_in[half, rows] * keep + mixed


def attend(first, n, info_ref, q_ref, *refs):
    chunks, refs = refs[:n], refs[n:]
    scratch, refs = refs[-4:], refs[:-4]
    state = (None,) * 3 + tuple(refs) if first else tuple(refs)
    own = info_ref[0]
    at = 1
    for c, chunk in enumerate(chunks):
        pairs = chunk.shape[0] // (2 * HALF)
        low = jnp.concatenate([chunk[i * 256 : i * 256 + 128] for i in range(pairs)], axis=0)
        high = jnp.concatenate([chunk[i * 256 + 128 : i * 256 + 256] for i in range(pairs)], axis=0)
        both = jnp.concatenate([low, high], axis=0)
        theirs = [info_ref[at + i] for i in range(pairs)]
        at += pairs
        if first:
            keeps = lambda seen: jnp.where(seen, 0.0, NEG)
            limit = lambda seen: jnp.where(seen, HALF, 0)
            below = [keeps(t <= own) for t in theirs]
            above = [keeps(t >= own) for t in theirs]
            below_limit = [limit(t != own) for t in theirs]
            high_offsets = [None] * pairs + above
            high_diagonal = [None] * pairs + below_limit
            low_diagonal = below_limit
        else:
            below = [jnp.where(t < own, 0.0, NEG) for t in theirs]
            high_offsets = [None] * pairs + [jnp.where(t > own, 0.0, NEG) for t in theirs]
            high_diagonal = low_diagonal = None
        work = []
        for t in range(ROWS // TILE):
            work.append((1, t, both, high_offsets, high_diagonal))
            work.append((0, t, low, below, low_diagonal))
        scored(q_ref, scratch[0], work[0][0], work[0][1], work[0][2][:, :128])
        scored(q_ref, scratch[1], work[1][0], work[1][1], work[1][2][:, :128])
        for i, (half, t, kv, offsets, diagonal) in enumerate(work):
            if i + 2 < len(work):
                h2, t2, kv2, _, _ = work[i + 2]
                scored(q_ref, scratch[(i + 2) % 4], h2, t2, kv2[:, :128])
            now = state if c == 0 else state[3:] * 2
            folded(
                scratch[i % 4], now, first and c == 0, half, t, kv[:, 128:], offsets, diagonal
            )


def attention(info, q, chunks, state):
    first = state is None
    n = len(chunks)
    tokens = sum(c.shape[0] for c in chunks)
    shape = jax.ShapeDtypeStruct((2, ROWS, HEAD_DIM), jnp.float32)
    vmem = pl.BlockSpec(memory_space=pltpu.VMEM)
    operands = (info, q, *chunks) + (() if first else tuple(state))
    return pl.pallas_call(
        functools.partial(attend, first, n),
        out_shape=(shape,) * 3,
        in_specs=[pl.BlockSpec(memory_space=pltpu.SMEM)] + [vmem] * (len(operands) - 1),
        out_specs=(vmem,) * 3,
        scratch_shapes=[
            pltpu.VMEM((TILE, HALF * width), jnp.float32) for width in (8, 4, 8, 4)
        ],
        input_output_aliases={} if first else {2 + n + k: k for k in range(3)},
        cost_estimate=pl.CostEstimate(
            flops=4 * ROWS * tokens * HEAD_DIM * 4,
            bytes_accessed=tokens * 512,
            transcendentals=ROWS * tokens,
        ),
        compiler_params=pltpu.CompilerParams(vmem_limit_bytes=48 * 1024 * 1024),
        name="attend_first" if first else "attend_next",
    )(*operands)


def finish(l_ref, a_ref, residual_ref, att_ref, own_ref):
    for half in range(2):
        for h in range(GROUP):
            rows = slice(h * HALF, (h + 1) * HALF)
            total = jnp.sum(l_ref[half, rows], axis=1, keepdims=True)
            att = a_ref[half, rows] / total
            to = (slice(half * HALF, (half + 1) * HALF), slice(h * HEAD_DIM, (h + 1) * HEAD_DIM))
            att_ref[to] = att
            own_ref[to] = (residual_ref[to].astype(jnp.float32) + att).astype(jnp.bfloat16)


def finished(totals, accum, residual):
    vmem = pl.BlockSpec(memory_space=pltpu.VMEM)
    return pl.pallas_call(
        finish,
        out_shape=(
            jax.ShapeDtypeStruct(residual.shape, jnp.float32),
            jax.ShapeDtypeStruct(residual.shape, jnp.bfloat16),
        ),
        in_specs=[vmem] * 3,
        out_specs=(vmem,) * 2,
        cost_estimate=pl.CostEstimate(flops=1 << 19, bytes_accessed=1 << 22, transcendentals=0),
        compiler_params=pltpu.CompilerParams(vmem_limit_bytes=32 * 1024 * 1024),
        name="finish",
    )(totals, accum, residual)


def body(queries, key_vectors, value_vectors, residual, pair_order, probe_gain, probe_weight):
    heads = 8
    nz, ny = lax.axis_size("z"), lax.axis_size("ylo")
    z = lax.axis_index("z")
    tokens = key_vectors.shape[1]

    k = key_vectors[0].reshape(tokens, heads, HEAD_DIM)
    v = value_vectors[0].reshape(tokens, heads, HEAD_DIM)
    kv = jnp.concatenate([k, v], axis=2).transpose(1, 0, 2)
    sent = jnp.broadcast_to(kv[None], (ny, heads, tokens, 2 * HEAD_DIM))
    sent = sent.reshape(ny * heads, tokens, 2 * HEAD_DIM)
    mine = lax.all_to_all(sent, ("ylo", *HEAD), split_axis=0, concat_axis=0, tiled=True)
    mine = mine.reshape(ny * heads * tokens, 2 * HEAD_DIM)

    q = queries[0].reshape(tokens, heads, GROUP * HEAD_DIM).transpose(1, 0, 2)

    def shift(x, by):
        return lax.ppermute(x, "z", [(i, (i + by) % nz) for i in range(nz)])

    left1, right1 = shift(mine, 1), shift(mine, -1)
    q = lax.all_to_all(q, HEAD, split_axis=0, concat_axis=0, tiled=True)
    q = q.reshape(2, HALF, GROUP, HEAD_DIM).transpose(0, 2, 1, 3).reshape(2, ROWS, HEAD_DIM)

    left2, right2 = shift(left1, 1), shift(right1, -1)
    left3, right3 = shift(left2, 1), shift(right2, -1)
    cut = left3.shape[0] // 2
    left4, right4 = shift(left3[:cut], 1), shift(right3[cut:], -1)

    table = pair_order.reshape(nz, ny)
    row = lax.broadcasted_iota(jnp.int32, (nz, ny), 0)
    column = lax.broadcasted_iota(jnp.int32, (nz, ny), 1)
    own = jnp.sum(jnp.where((row == z) & (column == lax.axis_index("ylo")), table, 0))

    def pairs_of(offset):
        return jnp.sum(jnp.where(row == (z + offset + nz) % nz, table, 0), axis=0)

    def info(*pieces):
        return jnp.concatenate([own[None], *pieces])

    state = attention(info(pairs_of(0)), q, (mine,), None)
    state = attention(info(pairs_of(-1), pairs_of(1)), q, (left1, right1), state)
    state = attention(info(pairs_of(-2), pairs_of(2)), q, (left2, right2), state)
    state = attention(info(pairs_of(-3), pairs_of(3)), q, (left3, right3), state)
    last = pairs_of(4)
    state = attention(info(last), q, (left4, right4), state)

    attended, own_stream = finished(state[1], state[2], residual)
    handed = lax.ppermute(own_stream, "section", [(0, 1)])
    later_stream = (handed.astype(jnp.float32) + attended).astype(jnp.bfloat16)
    stream = jnp.where(lax.axis_index("section") == 0, own_stream, later_stream)
    widened = stream.astype(jnp.float32)
    squares = jnp.sum(widened * widened, axis=-1)
    products = jnp.sum(widened * probe_gain[0][None, :] * probe_weight[0][None, :], axis=-1)
    both = jnp.stack([squares, products])
    copies = jnp.broadcast_to(both[None], (heads, *both.shape))
    both = jnp.sum(lax.all_to_all(copies, HEAD, split_axis=0, concat_axis=0, tiled=True), axis=0)
    reward = both[1] * lax.rsqrt(both[0] / D + 1e-05)
    return (stream[None], reward[None])


def solution(mesh):
    fine = Mesh(mesh.devices.reshape(2, 8, 4, 2, 4), ("section", "z", "ylo", "yhi", "x"))
    rows = ("z", "ylo", "yhi", "x")
    return jax.shard_map(
        body,
        mesh=fine,
        in_specs=(
            P("section", rows, None),
            P("section", rows, None),
            P("section", rows, None),
            P(("z", "ylo"), HEAD),
            P(),
            P("section", HEAD),
            P("section", HEAD),
        ),
        out_specs=(P("section", ("z", "ylo"), HEAD), P("section", ("z", "ylo"))),
        check_vma=False,
    )
```

```python
import functools
import math

import jax
import jax.numpy as jnp
from jax import lax
from jax.experimental import pallas as pl
from jax.experimental.pallas import tpu as pltpu
from jax.sharding import Mesh, PartitionSpec as P


D = 8192
HEADS = 64
KV_HEADS = 8
HEAD_DIM = 128
HALF = 128
GROUP = HEADS // KV_HEADS
ROWS = HALF * GROUP
TILE = 256

NEG = -1e30
SCALE = HEAD_DIM ** (-0.5) * math.log2(math.e)

HEAD = ("yhi", "x")


def scored(q_ref, s_ref, half, t, keys):
    rows = slice(t * TILE, (t + 1) * TILE)
    s_ref[:, : keys.shape[0]] = lax.dot_general(
        q_ref[half, rows], keys, (((1,), (1,)), ((), ())), preferred_element_type=jnp.float32
    )


def folded(s_ref, state, fresh, half, t, values, offsets, diagonal):
    rows = slice(t * TILE, (t + 1) * TILE)
    m_in, l_in, a_in, m_ref, l_ref, a_ref = state
    parts = []
    for j, offset in enumerate(offsets):
        p = s_ref[:, j * 128 : (j + 1) * 128]
        if offset is not None:
            p = p + offset
        if diagonal is not None and diagonal[j] is not None:
            r = lax.broadcasted_iota(jnp.int32, p.shape, 0) % HALF
            k = lax.broadcasted_iota(jnp.int32, p.shape, 1)
            p = jnp.where(k <= r + diagonal[j], p, NEG)
        parts.append(p)
    top = functools.reduce(jnp.maximum, parts)
    top = jnp.max(top, axis=1, keepdims=True)
    if fresh:
        new = jnp.broadcast_to(jnp.maximum(top, NEG), (TILE, 128))
    else:
        old = m_in[half, rows]
        new = jnp.maximum(old, top)
        keep = jnp.exp2((old - new) * SCALE)
    weights = [jnp.exp2((p - new) * SCALE) for p in parts]
    total = functools.reduce(jnp.add, weights)
    w = jnp.concatenate([p.astype(jnp.bfloat16) for p in weights], axis=1)
    mixed = jnp.dot(w, values, preferred_element_type=jnp.float32)
    m_ref[half, rows] = new
    if fresh:
        l_ref[half, rows] = total
        a_ref[half, rows] = mixed
    else:
        l_ref[half, rows] = l_in[half, rows] * keep + total
        a_ref[half, rows] = a_in[half, rows] * keep + mixed


def lower_blocks(info_ref, kind, step):
    z, _, section = (info_ref[i] for i in range(3))
    if step == 0:
        at, pairs = z * 4, 4
    elif step < 4:
        at, pairs = ((z + kind * step * (2 * section - 1) + 8) % 8) * 4, 4
    else:
        half = section if kind == 1 else 1 - section
        at, pairs = ((z + 4) % 8) * 4 + 2 * half, 2
    return [info_ref[3 + at + i] for i in range(pairs)]


def attend(first, origins, info_ref, q_ref, *refs):
    n = len(origins)
    chunks, refs = refs[:n], refs[n:]
    scratch, refs = refs[-4:], refs[:-4]
    state = (None,) * 3 + tuple(refs) if first else tuple(refs)
    own = info_ref[3 + info_ref[0] * 4 + info_ref[1]]
    for c, chunk in enumerate(chunks):
        theirs = lower_blocks(info_ref, *origins[c])
        pairs = len(theirs)
        low = jnp.concatenate([chunk[i * 256 : i * 256 + 128] for i in range(pairs)], axis=0)
        high = jnp.concatenate([chunk[i * 256 + 128 : i * 256 + 256] for i in range(pairs)], axis=0)
        both = jnp.concatenate([low, high], axis=0)
        if first:
            keeps = lambda seen: jnp.where(seen, 0.0, NEG)
            limit = lambda seen: jnp.where(seen, HALF, 0)
            below = [keeps(t <= own) for t in theirs]
            above = [keeps(t >= own) for t in theirs]
            below_limit = [limit(t != own) for t in theirs]
            high_offsets = [None] * pairs + above
            high_diagonal = [None] * pairs + below_limit
            low_diagonal = below_limit
        else:
            below = [jnp.where(t < own, 0.0, NEG) for t in theirs]
            high_offsets = [None] * pairs + [jnp.where(t > own, 0.0, NEG) for t in theirs]
            high_diagonal = low_diagonal = None
        work = []
        for t in range(ROWS // TILE):
            work.append((1, t, both, high_offsets, high_diagonal))
            work.append((0, t, low, below, low_diagonal))
        scored(q_ref, scratch[0], work[0][0], work[0][1], work[0][2][:, :128])
        scored(q_ref, scratch[1], work[1][0], work[1][1], work[1][2][:, :128])
        for i, (half, t, kv, offsets, diagonal) in enumerate(work):
            if i + 2 < len(work):
                h2, t2, kv2, _, _ = work[i + 2]
                scored(q_ref, scratch[(i + 2) % 4], h2, t2, kv2[:, :128])
            now = state if c == 0 else state[3:] * 2
            folded(
                scratch[i % 4], now, first and c == 0, half, t, kv[:, 128:], offsets, diagonal
            )


def attention(info, q, chunks, step, state):
    first = state is None
    n = len(chunks)
    origins = tuple((kind, step) for kind in (1, -1)[:n])
    tokens = 2 * HALF * n * (4 if step < 4 else 2)
    shape = jax.ShapeDtypeStruct((2, ROWS, HEAD_DIM), jnp.float32)
    vmem = pl.BlockSpec(memory_space=pltpu.VMEM)
    operands = (info, q, *chunks) + (() if first else tuple(state))
    return pl.pallas_call(
        functools.partial(attend, first, origins),
        out_shape=(shape,) * 3,
        in_specs=[pl.BlockSpec(memory_space=pltpu.SMEM)] + [vmem] * (len(operands) - 1),
        out_specs=(vmem,) * 3,
        scratch_shapes=[
            pltpu.VMEM((TILE, HALF * width), jnp.float32) for width in (8, 4, 8, 4)
        ],
        input_output_aliases={} if first else {2 + n + k: k for k in range(3)},
        cost_estimate=pl.CostEstimate(
            flops=4 * ROWS * tokens * HEAD_DIM * 4,
            bytes_accessed=tokens * 512,
            transcendentals=ROWS * tokens,
        ),
        compiler_params=pltpu.CompilerParams(vmem_limit_bytes=16 * 1024 * 1024),
        name="attend_first" if first else "attend_next",
    )(*operands)


def finish(l_ref, a_ref, residual_ref, att_ref, own_ref):
    for half in range(2):
        for h in range(GROUP):
            rows = slice(h * HALF, (h + 1) * HALF)
            total = jnp.sum(l_ref[half, rows], axis=1, keepdims=True)
            att = a_ref[half, rows] / total
            to = (slice(half * HALF, (half + 1) * HALF), slice(h * HEAD_DIM, (h + 1) * HEAD_DIM))
            att_ref[to] = att
            own_ref[to] = (residual_ref[to].astype(jnp.float32) + att).astype(jnp.bfloat16)


def finished(totals, accum, residual):
    vmem = pl.BlockSpec(memory_space=pltpu.VMEM)
    return pl.pallas_call(
        finish,
        out_shape=(
            jax.ShapeDtypeStruct(residual.shape, jnp.float32),
            jax.ShapeDtypeStruct(residual.shape, jnp.bfloat16),
        ),
        in_specs=[vmem] * 3,
        out_specs=(vmem,) * 2,
        cost_estimate=pl.CostEstimate(flops=1 << 19, bytes_accessed=1 << 22, transcendentals=0),
        compiler_params=pltpu.CompilerParams(vmem_limit_bytes=8 * 1024 * 1024),
        name="finish",
    )(totals, accum, residual)


def sublayers(queries, key_vectors, value_vectors, residual, pair_order, probe_gain, probe_weight):
    heads = 8
    nz, ny = lax.axis_size("z"), lax.axis_size("ylo")
    z = lax.axis_index("z")
    tokens = key_vectors.shape[1]

    k = key_vectors[0].reshape(tokens, heads, HEAD_DIM)
    v = value_vectors[0].reshape(tokens, heads, HEAD_DIM)
    kv = jnp.concatenate([k, v], axis=2).transpose(1, 0, 2)
    sent = jnp.broadcast_to(kv[None], (ny, heads, tokens, 2 * HEAD_DIM))
    sent = sent.reshape(ny * heads, tokens, 2 * HEAD_DIM)
    mine = lax.all_to_all(sent, ("ylo", *HEAD), split_axis=0, concat_axis=0, tiled=True)
    mine = mine.reshape(ny * heads * tokens, 2 * HEAD_DIM)

    q = queries[0].reshape(tokens, heads, GROUP * HEAD_DIM).transpose(1, 0, 2)

    section = lax.axis_index("section")
    onward = [(i, (i + 1) % nz) for i in range(nz)]
    onward += [(nz + i, nz + (i - 1) % nz) for i in range(nz)]

    def passed(x):
        return lax.ppermute(x, ("section", "z"), onward)

    def swapped(x):
        return lax.ppermute(x, "section", [(0, 1), (1, 0)])

    count = mine.shape[0]
    packet = jnp.concatenate([mine, swapped(mine)], axis=0)
    packet1 = passed(packet)
    q = lax.all_to_all(q, HEAD, split_axis=0, concat_axis=0, tiled=True)
    q = q.reshape(2, HALF, GROUP, HEAD_DIM).transpose(0, 2, 1, 3).reshape(2, ROWS, HEAD_DIM)
    packet2 = passed(packet1)
    across1 = swapped(packet1[count:])
    packet3 = passed(packet2)
    across2 = swapped(packet2[count:])
    part = lax.dynamic_index_in_dim(
        packet3.reshape(2, 2, count // 2, 2 * HEAD_DIM), section, axis=1, keepdims=False
    )
    packet4 = passed(part.reshape(count, 2 * HEAD_DIM))
    across3 = swapped(packet3[count:])
    across4 = swapped(packet4[count // 2 :])

    here = jnp.stack([z, lax.axis_index("ylo"), section]).astype(jnp.int32)
    info = jnp.concatenate([here, pair_order])
    chunks = ((mine,), (packet1, across1), (packet2, across2), (packet3, across3), (packet4, across4))
    state = None
    for i, arrived in enumerate(chunks):
        state = attention(info, q, arrived, i, state)

    attended, own_stream = finished(state[1], state[2], residual)
    handed = lax.ppermute(own_stream, "section", [(0, 1)])
    later_stream = (handed.astype(jnp.float32) + attended).astype(jnp.bfloat16)
    stream = jnp.where(section == 0, own_stream, later_stream)
    widened = stream.astype(jnp.float32)
    squares = jnp.sum(widened * widened, axis=-1)
    products = jnp.sum(widened * probe_gain[0][None, :] * probe_weight[0][None, :], axis=-1)
    both = jnp.stack([squares, products])
    copies = jnp.broadcast_to(both[None], (heads, *both.shape))
    both = jnp.sum(lax.all_to_all(copies, HEAD, split_axis=0, concat_axis=0, tiled=True), axis=0)
    reward = both[1] * lax.rsqrt(both[0] / D + 1e-05)
    return (stream[None], reward[None])


def solution(mesh):
    fine = Mesh(mesh.devices.reshape(2, 8, 4, 2, 4), ("section", "z", "ylo", "yhi", "x"))
    rows = ("z", "ylo", "yhi", "x")
    return jax.shard_map(
        sublayers,
        mesh=fine,
        in_specs=(
            P("section", rows, None),
            P("section", rows, None),
            P("section", rows, None),
            P(("z", "ylo"), HEAD),
            P(),
            P("section", HEAD),
            P("section", HEAD),
        ),
        out_specs=(P("section", ("z", "ylo"), HEAD), P("section", ("z", "ylo"))),
        check_vma=False,
    )
```
